32 devices in a mesh: dp: 32 (over z, y, x, core).
Axes of the slice: x: 2, y: 2, z: 4, core: 2. Of those that a mesh axis runs over, the one named last changes fastest.
Arguments:
- params: float32 [1774080], P('dp')
- images: bfloat16 [256, 197, 384], P('dp'), may hold values from -6 to 6
- cotangent: bfloat16 [256, 197, 384], P('dp'), may hold values from -6 to 6
- live: int32 [32], P('dp'), may hold values from 1 to 8, as said below
Outputs:
- layer_out: bfloat16 [256, 197, 384], P('dp')
- input_grad: bfloat16 [256, 197, 384], P('dp')
- flat_parameter_gradient: float32 [1774080], P('dp')
The draws below stay inside these ranges and needn't reach their ends.
Inputs may be any that keep to these rules, and one draw needn't show every extreme that they name: The first live[d] of device d's 8 slots hold images; every draw has a device with all 8 slots occupied.
All inputs are finite; a program needn't handle non-finite values.
Results may differ from the reference program's by a relative error of at most 0.0098.
Values may be sent and summed in bfloat16 or wider, within the bound.
A program may use at most 192 MiB of HBM per device.

```python
import jax
import jax.numpy as jnp
from jax import lax

D = 384
HEADS = 6
FF = 1536
TOK = 197
IMG_DEV = 8
SLOTS = 256
PARAMS = 1774080
N_DP = 32


def draw_params(key, part):
    subkeys = jax.random.split(key, 16)

    def rough_draw(number, count, scale):
        return jax.random.normal(subkeys[number], (count,), jnp.float32) * scale

    def gain_draw(number):
        return 1.0 + 0.4 * jax.random.uniform(subkeys[number], (D,), jnp.float32, -1.0, 1.0)
    w_qkv = rough_draw(2, D * 3 * D, D ** (-0.5)).reshape(D, 3 * D)
    pieces = [gain_draw(0), rough_draw(1, D, 0.3), w_qkv.reshape(-1), rough_draw(3, D, 0.3), rough_draw(4, D, 0.3), rough_draw(5, D * D, 3.0 * D ** (-0.5)), rough_draw(6, D, 0.3), gain_draw(7), rough_draw(8, D, 0.3), rough_draw(9, D * FF, D ** (-0.5)), rough_draw(10, FF, 0.3), rough_draw(11, FF * D, FF ** (-0.5)), rough_draw(12, D, 0.3)]
    used = 4 * D * D + 2 * D * FF + 8 * D + FF
    pieces.append(rough_draw(13, PARAMS - used, 1.0))
    return jnp.concatenate(pieces)


def draw_live(key, part):
    devices = SLOTS // IMG_DEV
    counts = jax.random.randint(jax.random.fold_in(key, 1), (devices,), 1, IMG_DEV + 1)
    chosen = jax.random.randint(jax.random.fold_in(key, 2), (), 0, devices)
    return counts.at[chosen].set(IMG_DEV).astype(jnp.int32)


def steps_of(key, shape, cuts, low, high):
    loudness = 1.0
    for dim, parts in cuts:
        heights = jax.random.uniform(jax.random.fold_in(jax.random.fold_in(key, 6), dim), (parts,), jnp.float32, low / len(cuts), high / len(cuts))
        loudness = loudness * jnp.repeat(jnp.exp(heights), shape[dim] // parts).reshape((-1,) + (1,) * (len(shape) - 1 - dim))
    return loudness


def gaussian(key, shape, scale, most, shards=(), kind=jnp.bfloat16):
    entries = jax.random.normal(key, shape, jnp.float32) * scale
    if len(shards) > 0:
        entries = steps_of(key, shape, shards, -0.22, 0.18) * entries
    return jnp.clip(entries, min=-most, max=most).astype(kind)


def setup_inputs(seed: int = 0) -> dict:
    arg_keys = jax.random.split(jax.random.key(seed), 5)
    return {
        "params": draw_params(jax.random.fold_in(arg_keys[4], 71), 0),
        "images": gaussian(arg_keys[1], (SLOTS, TOK, D), 1.0, 6.0, ((0, 32),)),
        "cotangent": gaussian(arg_keys[2], (SLOTS, TOK, D), 1.0, 6.0, ((0, 32),)),
        "live": draw_live(jax.random.fold_in(arg_keys[4], 71), 0),
    }


EPS = 1e-06

def norm_rows(values, gain, shift):
    center = values - lax.optimization_barrier(jnp.mean(values, axis=-1, keepdims=True))
    inv_std = lax.rsqrt(lax.optimization_barrier(jnp.mean(center * center, axis=-1, keepdims=True)) + EPS)
    normed = center * inv_std
    return (normed * gain + shift, normed, inv_std)

def norm_back(grad_out, normed, inv_std, gain):
    grad_hat = grad_out * gain
    return inv_std * (grad_hat - lax.optimization_barrier(jnp.mean(grad_hat, axis=-1, keepdims=True)) - normed * lax.optimization_barrier(jnp.mean(grad_hat * normed, axis=-1, keepdims=True)))

def unpack(weights):
    widths = [D, D, D * 3 * D, D, D, D * D, D, D, D, D * FF, FF, FF * D, D]
    pieces = []
    start = 0
    for width in widths:
        pieces.append(weights[start:start + width])
        start = start + width
    pieces[2] = pieces[2].reshape(D, 3 * D)
    pieces[5] = pieces[5].reshape(D, D)
    pieces[9] = pieces[9].reshape(D, FF)
    pieces[11] = pieces[11].reshape(FF, D)
    return pieces

def forward_sweep(weights, images):
    gain_one, shift_one, w_qkv, bias_q, bias_v, w_out, bias_out, gain_two, shift_two, w_up, bias_up, w_down, bias_down = unpack(weights)
    batch, length = (images.shape[0], images.shape[1])
    head_dim = D // HEADS
    inputs = images.astype(jnp.float32)
    normed_one, hat_one, inv_one = norm_rows(inputs, gain_one, shift_one)
    attn_in = normed_one.astype(jnp.bfloat16)
    bias_all = jnp.concatenate([bias_q, jnp.zeros_like(bias_q), bias_v]).astype(jnp.float32)
    project = jnp.einsum('btd,de->bte', attn_in, w_qkv, preferred_element_type=jnp.float32) + bias_all
    batched_projection = project.astype(jnp.bfloat16)
    query = batched_projection[..., :D].reshape(batch, length, HEADS, head_dim)
    keys_all = batched_projection[..., D:2 * D].reshape(batch, length, HEADS, head_dim)
    values_all = batched_projection[..., 2 * D:].reshape(batch, length, HEADS, head_dim)
    scale = head_dim ** (-0.5)
    scores = jnp.einsum('bqhd,bkhd->bhqk', query, keys_all, preferred_element_type=jnp.float32) * scale
    log_total = jax.nn.logsumexp(scores, axis=-1)
    probs_b = jnp.exp(scores - log_total[..., None]).astype(jnp.bfloat16)
    mixed = jnp.einsum('bhqk,bkhd->bqhd', probs_b, values_all, preferred_element_type=jnp.float32)
    mixed_b = mixed.reshape(batch, length, D).astype(jnp.bfloat16)
    hidden = inputs + jnp.einsum('btd,de->bte', mixed_b, w_out, preferred_element_type=jnp.float32) + bias_out.astype(jnp.float32)
    normed_two, hat_two, inverse_std_second = norm_rows(hidden, gain_two, shift_two)
    ffn_in = normed_two.astype(jnp.bfloat16)
    pre_act = jnp.einsum('btd,df->btf', ffn_in, w_up, preferred_element_type=jnp.float32) + bias_up.astype(jnp.float32)
    act_b = jax.nn.gelu(pre_act, approximate=False).astype(jnp.bfloat16)
    result = hidden + jnp.einsum('btf,fd->btd', act_b, w_down, preferred_element_type=jnp.float32) + bias_down.astype(jnp.float32)
    saved_activation = (hat_one, inv_one, attn_in, batched_projection, log_total, mixed_b, hat_two, inverse_std_second, ffn_in, pre_act, act_b)
    return (result, saved_activation)

def reverse_sweep(weights, saved_activation, cotangent, mask):
    gain_one, shift_one, w_qkv, bias_q, bias_v, w_out, bias_out, gain_two, shift_two, w_up, bias_up, w_down, bias_down = unpack(weights)
    hat_one, inv_one, attn_in, batched_projection, log_total, mixed_b, hat_two, inverse_std_second, ffn_in, pre_act, act_b = saved_activation
    batch, length = (cotangent.shape[0], cotangent.shape[1])
    head_dim = D // HEADS
    scale = head_dim ** (-0.5)
    dout = cotangent.astype(jnp.float32) * mask[:, None, None]
    dout_b = dout.astype(jnp.bfloat16)
    grad_down = jnp.einsum('btf,btd->fd', act_b, dout_b, preferred_element_type=jnp.float32)
    grad_bias_down = lax.optimization_barrier(jnp.sum(dout, axis=(0, 1)))
    dact = jnp.einsum('btd,fd->btf', dout_b, w_down, preferred_element_type=jnp.float32)
    cumul = 0.5 * (1.0 + lax.erf(pre_act * 0.7071067811865476))
    density = jnp.exp(-0.5 * pre_act * pre_act) * 0.3989422804014327
    dpre = dact * (cumul + pre_act * density)
    dpre_b = dpre.astype(jnp.bfloat16)
    grad_up = jnp.einsum('btd,btf->df', ffn_in, dpre_b, preferred_element_type=jnp.float32)
    grad_bias_up = lax.optimization_barrier(jnp.sum(dpre, axis=(0, 1)))
    dnorm_two = jnp.einsum('btf,df->btd', dpre_b, w_up, preferred_element_type=jnp.float32)
    grad_gain_two = lax.optimization_barrier(jnp.sum(dnorm_two * hat_two, axis=(0, 1)))
    grad_shift_two = lax.optimization_barrier(jnp.sum(dnorm_two, axis=(0, 1)))
    dhidden = dout + norm_back(dnorm_two, hat_two, inverse_std_second, gain_two)
    dhidden_b = dhidden.astype(jnp.bfloat16)
    grad_out = jnp.einsum('btd,bte->de', mixed_b, dhidden_b, preferred_element_type=jnp.float32)
    grad_bias_out = lax.optimization_barrier(jnp.sum(dhidden, axis=(0, 1)))
    dmixed = jnp.einsum('bte,de->btd', dhidden_b, w_out, preferred_element_type=jnp.float32)
    dmixed_b = dmixed.astype(jnp.bfloat16).reshape(batch, length, HEADS, head_dim)
    query = batched_projection[..., :D].reshape(batch, length, HEADS, head_dim)
    keys_all = batched_projection[..., D:2 * D].reshape(batch, length, HEADS, head_dim)
    values_all = batched_projection[..., 2 * D:].reshape(batch, length, HEADS, head_dim)
    scores = jnp.einsum('bqhd,bkhd->bhqk', query, keys_all, preferred_element_type=jnp.float32) * scale
    probs = jnp.exp(scores - log_total[..., None])
    probs_b = probs.astype(jnp.bfloat16)
    dvalue = jnp.einsum('bhqk,bqhd->bkhd', probs_b, dmixed_b, preferred_element_type=jnp.float32)
    dprobs = jnp.einsum('bqhd,bkhd->bhqk', dmixed_b, values_all, preferred_element_type=jnp.float32)
    delta = lax.optimization_barrier(jnp.sum(probs * dprobs, axis=-1, keepdims=True))
    dscores_b = (probs * (dprobs - delta) * scale).astype(jnp.bfloat16)
    dquery = jnp.einsum('bhqk,bkhd->bqhd', dscores_b, keys_all, preferred_element_type=jnp.float32)
    dkey = jnp.einsum('bhqk,bqhd->bkhd', dscores_b, query, preferred_element_type=jnp.float32)
    dqkv = jnp.concatenate([dquery.reshape(batch, length, D), dkey.reshape(batch, length, D), dvalue.reshape(batch, length, D)], axis=-1)
    dqkv_b = dqkv.astype(jnp.bfloat16)
    grad_qkv = jnp.einsum('btd,bte->de', attn_in, dqkv_b, preferred_element_type=jnp.float32)
    grad_bias_q = lax.optimization_barrier(jnp.sum(dqkv[..., :D], axis=(0, 1)))
    grad_bias_v = lax.optimization_barrier(jnp.sum(dqkv[..., 2 * D:], axis=(0, 1)))
    dnorm_one = jnp.einsum('bte,de->btd', dqkv_b, w_qkv, preferred_element_type=jnp.float32)
    grad_gain_one = lax.optimization_barrier(jnp.sum(dnorm_one * hat_one, axis=(0, 1)))
    grad_shift_one = lax.optimization_barrier(jnp.sum(dnorm_one, axis=(0, 1)))
    dinput = dhidden + norm_back(dnorm_one, hat_one, inv_one, gain_one)
    pieces = [grad_gain_one, grad_shift_one, grad_qkv, grad_bias_q, grad_bias_v, grad_out, grad_bias_out, grad_gain_two, grad_shift_two, grad_up, grad_bias_up, grad_down, grad_bias_down]
    flat = jnp.concatenate([piece.reshape(-1) for piece in pieces])
    padding = jnp.zeros((weights.shape[0] - flat.shape[0],), jnp.float32)
    return (dinput.astype(jnp.bfloat16), jnp.concatenate([flat, padding]))

def reference(params, images, cotangent, live):
    weights = params.astype(jnp.bfloat16)
    masks = (jnp.arange(IMG_DEV, dtype=jnp.int32)[None, :] < live[:, None]).astype(jnp.float32)
    image_blocks = images.reshape(N_DP, IMG_DEV, TOK, D)
    cot_blocks = cotangent.reshape(N_DP, IMG_DEV, TOK, D)

    def step_block(total, block):
        image_block, cot_block, mask_block = block
        result, saved_activation = forward_sweep(weights, image_block)
        output = (result * mask_block[:, None, None]).astype(jnp.bfloat16)
        dinput, grads = reverse_sweep(weights, saved_activation, cot_block, mask_block)
        return (total + grads, (output, dinput))
    start = jnp.zeros((params.shape[0],), jnp.float32)
    total, (outputs, dinputs) = lax.scan(step_block, start, (image_blocks, cot_blocks, masks))
    return (outputs.reshape(SLOTS, TOK, D), dinputs.reshape(SLOTS, TOK, D), total)
```

```python
import functools

import jax
import jax.numpy as jnp
from jax import lax
from jax.experimental import pallas as pl
from jax.experimental.pallas import tpu as pltpu
from jax.sharding import PartitionSpec as P

D = 384
HEADS = 6
FF = 1536
HD = D // HEADS
PAIRS = HEADS // 2
EPS = 1e-06
LANES = 128
BF = jnp.bfloat16
F32 = jnp.float32

ROW_QKV = 2
ROW_OUT = 2 + 3 * D + 2
ROW_UP = ROW_OUT + D + 3
ROW_BUP = ROW_UP + FF
ROW_DOWN = ROW_BUP + FF // D
ROW_BDOWN = ROW_DOWN + FF
ROWS = ROW_BDOWN + 1
VEC_ROWS = (0, 1, ROW_OUT - 2, ROW_OUT - 1, ROW_UP - 3, ROW_UP - 2, ROW_UP - 1, ROW_BDOWN)
G1, S1, BQ, BV, BO, G2, S2, BD = range(8)

GROUP = 2
CHUNK = 512


def up_to(value, unit):
    return (value + unit - 1) // unit * unit


def nt(a, b):
    return lax.dot_general(a, b, (((1,), (1,)), ((), ())), preferred_element_type=F32)


def tn(a, b):
    return lax.dot_general(a, b, (((0,), (0,)), ((), ())), preferred_element_type=F32)


def nn(a, b):
    return jnp.dot(a, b, preferred_element_type=F32)


def norm_stats(values):
    center = values - jnp.mean(values, axis=-1, keepdims=True)
    inv = lax.rsqrt(jnp.mean(center * center, axis=-1, keepdims=True) + EPS)
    return center * inv, inv


def norm_back(grad_out, hat, inv, gain):
    g = grad_out * gain
    return inv * (
        g
        - jnp.mean(g, axis=-1, keepdims=True)
        - hat * jnp.mean(g * hat, axis=-1, keepdims=True)
    )


def colsum(v):
    return jnp.sum(v, axis=0, keepdims=True)


def matrices():
    return (
        (0, D, 9, ROW_QKV),
        (1, D, 3, ROW_OUT),
        (2, D, 12, ROW_UP),
        (3, FF, 3, ROW_DOWN),
    )


def layer_kernel(
    n, shard, tok, tokp,
    live_ref, gath_ref, img_ref, cot_ref,
    out_ref, din_ref, grad_ref,
    buf, wqkv, wout, wup, wdn, vec, bup,
    gqkv, gout, gup, gdn, gvec, gbup,
    x_s, dout_s, attn_s, qkv_s, probs_s, mixed_s, dmix_s, dqkv_s,
):
    step = pl.program_id(0)
    window = gath_ref.shape[1]
    weights = (wqkv, wout, wup, wdn)
    grads = (gqkv, gout, gup, gdn)

    @pl.when(step == 0)
    def _():
        for d in range(n):
            first, shift = divmod(shard * d, LANES)
            rows = (shift + shard + LANES - 1) // LANES
            piece = gath_ref[d].astype(F32)
            if d > 0 and shift:
                seam = buf[first : first + 1, :] + piece[0:1]
                buf[first : first + rows, :] = piece[:rows]
                buf[first : first + 1, :] = seam
            else:
                buf[first : first + rows, :] = piece[:rows]
        for k, rows, blocks, start in matrices():
            for b in range(blocks):
                weights[k][:, b * LANES : (b + 1) * LANES] = buf[
                    pl.ds(3 * start + b, rows, blocks), :
                ].astype(BF)
        for i, r in enumerate(VEC_ROWS):
            for c in range(3):
                vec[i : i + 1, c * LANES : (c + 1) * LANES] = buf[3 * r + c : 3 * r + c + 1, :]
        for c in range(FF // LANES):
            bup[:, c * LANES : (c + 1) * LANES] = buf[3 * ROW_BUP + c : 3 * ROW_BUP + c + 1, :]
        for ref in (*grads, gvec, gbup, x_s, dout_s):
            ref[...] = jnp.zeros_like(ref)

    def param(i):
        return vec[i : i + 1, :]

    def add_vec(i, value):
        gvec[i : i + 1, :] += value

    live = live_ref[0]
    masks = [(step * GROUP + g < live).astype(F32) for g in range(GROUP)]
    for g in range(GROUP):
        x_s[g * tokp : g * tokp + tok, :] = img_ref[g].astype(F32)
        dout_s[g * tokp : g * tokp + tok, :] = cot_ref[g].astype(F32) * masks[g]

    hat1, _ = norm_stats(x_s[...])
    attn_s[...] = (hat1 * param(G1) + param(S1)).astype(BF)
    attn_in = attn_s[...]
    for j, bias in enumerate((BQ, None, BV)):
        part = nn(attn_in, wqkv[:, j * D : (j + 1) * D])
        if bias is not None:
            part = part + param(bias)
        qkv_s[:, j * D : (j + 1) * D] = part.astype(BF)

    lane = lax.broadcasted_iota(jnp.int32, (1, LANES), 1)
    low = lane < HD
    low_b = low.astype(BF)
    high_b = 1 - low_b
    key_ok = lax.broadcasted_iota(jnp.int32, (1, tokp), 1) < tok

    def views(t):
        g, p = t // PAIRS, t % PAIRS
        rows = pl.ds(pl.multiple_of(g * tokp, 16), tokp)
        return rows, [pl.ds(pl.multiple_of(j * D + p * LANES, LANES), LANES) for j in range(3)]

    def stack(v):
        return jnp.concatenate([v * low_b, v * high_b], axis=0)

    def attend(t, carry):
        rows, (cq, ck, cv) = views(t)
        q, k, v = qkv_s[rows, cq], qkv_s[rows, ck], qkv_s[rows, cv]
        s = nt(stack(q), k) * (HD**-0.5)
        s = jnp.where(key_ok, s, -1e30)
        e = jnp.exp(s - jnp.max(s, axis=-1, keepdims=True))
        probs = e * (1.0 / jnp.sum(e, axis=-1, keepdims=True))
        probs_s[t] = probs
        mixed = nn(probs.astype(BF), v)
        mixed_s[rows, cq] = jnp.where(low, mixed[:tokp], mixed[tokp:]).astype(BF)
        return carry

    lax.fori_loop(0, GROUP * PAIRS, attend, 0)

    hidden = x_s[...] + nn(mixed_s[...], wout[...]) + param(BO)
    hat2, inv2 = norm_stats(hidden)
    ffn_in = (hat2 * param(G2) + param(S2)).astype(BF)
    dout = dout_s[...]
    dout_b = dout.astype(BF)
    add_vec(BD, colsum(dout))
    result = hidden + param(BD)
    dn2 = jnp.zeros_like(hidden)
    for c in range(FF // CHUNK):
        cols = slice(c * CHUNK, (c + 1) * CHUNK)
        pre = nn(ffn_in, wup[:, cols]) + bup[:, cols]
        cumul = 0.5 * (1.0 + lax.erf(pre * 0.7071067811865476))
        act = (pre * cumul).astype(BF)
        result = result + nn(act, wdn[cols, :])
        gdn[cols, :] += tn(act, dout_b)
        density = jnp.exp(-0.5 * pre * pre) * 0.3989422804014327
        dpre = nt(dout_b, wdn[cols, :]) * (cumul + pre * density)
        gbup[:, cols] += colsum(dpre)
        dpre_b = dpre.astype(BF)
        gup[:, cols] += tn(ffn_in, dpre_b)
        dn2 = dn2 + nt(dpre_b, wup[:, cols])
    for g in range(GROUP):
        out_ref[g] = (result[g * tokp : g * tokp + tok] * masks[g]).astype(BF)

    add_vec(G2, colsum(dn2 * hat2))
    add_vec(S2, colsum(dn2))
    dhidden = dout + norm_back(dn2, hat2, inv2, param(G2))
    dout_s[...] = dhidden
    dhidden_b = dhidden.astype(BF)
    add_vec(BO, colsum(dhidden))
    gout[...] += tn(mixed_s[...], dhidden_b)
    dmix_s[...] = nt(dhidden_b, wout[...]).astype(BF)

    def attend_back(t, carry):
        rows, (cq, ck, cv) = views(t)
        q, k, v = qkv_s[rows, cq], qkv_s[rows, ck], qkv_s[rows, cv]
        dm = stack(dmix_s[rows, cq])
        probs = probs_s[t]
        dprobs = nt(dm, v)
        delta = jnp.sum(probs * dprobs, axis=-1, keepdims=True)
        ds = (probs * (dprobs - delta) * (HD**-0.5)).astype(BF)
        dvalue = tn(probs.astype(BF), dm)
        dq = nn(ds, k)
        dquery = jnp.where(low, dq[:tokp], dq[tokp:])
        dkey = tn(ds, stack(q))
        gvec[BQ : BQ + 1, cq] += colsum(dquery)
        gvec[BV : BV + 1, cq] += colsum(dvalue)
        dqkv_s[rows, cq] = dquery.astype(BF)
        dqkv_s[rows, ck] = dkey.astype(BF)
        dqkv_s[rows, cv] = dvalue.astype(BF)
        return carry

    lax.fori_loop(0, GROUP * PAIRS, attend_back, 0)

    attn_in = attn_s[...]
    dn1 = jnp.zeros_like(hidden)
    for j in range(3):
        cols = slice(j * D, (j + 1) * D)
        part = dqkv_s[:, cols]
        gqkv[:, cols] += tn(attn_in, part)
        dn1 = dn1 + nt(part, wqkv[:, cols])
    hat1, inv1 = norm_stats(x_s[...])
    add_vec(G1, colsum(dn1 * hat1))
    add_vec(S1, colsum(dn1))
    dinput = dout_s[...] + norm_back(dn1, hat1, inv1, param(G1))
    for g in range(GROUP):
        din_ref[g] = dinput[g * tokp : g * tokp + tok].astype(BF)
        dout_s[g * tokp + tok : (g + 1) * tokp, :] = jnp.zeros((tokp - tok, D), F32)

    @pl.when(step == pl.num_programs(0) - 1)
    def _():
        for k, rows, blocks, start in matrices():
            for b in range(blocks):
                buf[pl.ds(3 * start + b, rows, blocks), :] = grads[k][
                    :, b * LANES : (b + 1) * LANES
                ]
        for i, r in enumerate(VEC_ROWS):
            for c in range(3):
                buf[3 * r + c : 3 * r + c + 1, :] = gvec[i : i + 1, c * LANES : (c + 1) * LANES]
        for c in range(FF // LANES):
            buf[3 * ROW_BUP + c : 3 * ROW_BUP + c + 1, :] = gbup[:, c * LANES : (c + 1) * LANES]
        tail = buf.shape[0] - 3 * ROWS
        buf[3 * ROWS :, :] = jnp.zeros((tail, LANES), F32)
        for d in range(n):
            first = shard * d // LANES
            grad_ref[d] = buf[first : first + window, :].astype(grad_ref.dtype)


def run_layer(n, shard, window, live, gathered, images, cotangent):
    slots, tok, _ = images.shape
    tokp = up_to(tok, 16)
    rows = GROUP * tokp
    buf_rows = up_to(max(shard * (n - 1) // LANES + window, 3 * ROWS) + 8, 8)
    block = pl.BlockSpec((GROUP, tok, D), lambda i: (i, 0, 0))
    whole = pl.BlockSpec(memory_space=pltpu.VMEM)
    VM = pltpu.VMEM
    return pl.pallas_call(
        functools.partial(layer_kernel, n, shard, tok, tokp),
        grid=(slots // GROUP,),
        in_specs=[pl.BlockSpec(memory_space=pltpu.SMEM), whole, block, block],
        out_specs=[block, block, whole],
        out_shape=[
            jax.ShapeDtypeStruct(images.shape, BF),
            jax.ShapeDtypeStruct(images.shape, BF),
            jax.ShapeDtypeStruct((n, window, LANES), BF),
        ],
        scratch_shapes=[
            VM((buf_rows, LANES), F32),
            VM((D, 3 * D), BF), VM((D, D), BF), VM((D, FF), BF), VM((FF, D), BF),
            VM((8, D), F32), VM((1, FF), F32),
            VM((D, 3 * D), F32), VM((D, D), F32), VM((D, FF), F32), VM((FF, D), F32),
            VM((8, D), F32), VM((1, FF), F32),
            VM((rows, D), F32), VM((rows, D), F32), VM((rows, D), BF),
            VM((rows, 3 * D), BF), VM((GROUP * PAIRS, 2 * tokp, tokp), F32),
            VM((rows, D), BF), VM((rows, D), BF), VM((rows, 3 * D), BF),
        ],
        compiler_params=pltpu.CompilerParams(
            dimension_semantics=("arbitrary",), vmem_limit_bytes=63 * 1024 * 1024
        ),
        name="layer",
    )(live, gathered, images, cotangent)


def shards(params, images, cotangent, live):
    n = lax.axis_size("dp")
    shard = params.shape[0]
    window = up_to((shard + 2 * LANES - 2) // LANES, 16)
    me = lax.axis_index("dp")
    shift = (shard % LANES) * me % LANES
    padded = jnp.pad(params, (0, window * LANES - shard))
    moved = jnp.roll(padded, shift).astype(BF).reshape(window, LANES)
    gathered = lax.all_gather(moved, "dp", axis=0)
    out, din, grads = run_layer(n, shard, window, live, gathered, images, cotangent)
    mine = lax.psum_scatter(
        grads.reshape(n * window, LANES), "dp", scatter_dimension=0, tiled=True
    )
    flat = lax.dynamic_slice(mine.astype(F32).reshape(-1), (shift,), (shard,))
    return out, din, flat


def solution(mesh):
    return jax.shard_map(
        shards,
        mesh=mesh,
        in_specs=(P("dp"), P("dp", None, None), P("dp", None, None), P("dp")),
        out_specs=(P("dp", None, None), P("dp", None, None), P("dp")),
        check_vma=False,
    )
```

```python
import functools

import jax
import jax.numpy as jnp
from jax import lax
from jax.experimental import pallas as pl
from jax.experimental.pallas import tpu as pltpu
from jax.sharding import PartitionSpec as P

D = 384
HEADS = 6
FF = 1536
HD = D // HEADS
PAIRS = HEADS // 2
EPS = 1e-06
LANES = 128
BF = jnp.bfloat16
F32 = jnp.float32

ROW_QKV = 2
ROW_OUT = 2 + 3 * D + 2
ROW_UP = ROW_OUT + D + 3
ROW_BUP = ROW_UP + FF
ROW_DOWN = ROW_BUP + FF // D
ROW_BDOWN = ROW_DOWN + FF
ROWS = ROW_BDOWN + 1
VEC_ROWS = (0, 1, ROW_OUT - 2, ROW_OUT - 1, ROW_UP - 3, ROW_UP - 2, ROW_UP - 1, ROW_BDOWN)
G1, S1, BQ, BV, BO, G2, S2, BD = range(8)

GROUP = 2
CHUNK = 512


def up_to(value, unit):
    return (value + unit - 1) // unit * unit


def nt(a, b):
    return lax.dot_general(a, b, (((1,), (1,)), ((), ())), preferred_element_type=F32)


def tn(a, b):
    return lax.dot_general(a, b, (((0,), (0,)), ((), ())), preferred_element_type=F32)


def nn(a, b):
    return jnp.dot(a, b, preferred_element_type=F32)


def norm_stats(values):
    center = values - jnp.mean(values, axis=-1, keepdims=True)
    inv = lax.rsqrt(jnp.mean(center * center, axis=-1, keepdims=True) + EPS)
    return center * inv, inv


def norm_back(grad_out, hat, inv, gain):
    g = grad_out * gain
    return inv * (
        g
        - jnp.mean(g, axis=-1, keepdims=True)
        - hat * jnp.mean(g * hat, axis=-1, keepdims=True)
    )


def colsum(v):
    return jnp.sum(v, axis=0, keepdims=True)


def matrices():
    return (
        (0, D, 9, ROW_QKV),
        (1, D, 3, ROW_OUT),
        (2, D, 12, ROW_UP),
        (3, FF, 3, ROW_DOWN),
    )


def layer_kernel(
    n, shard, tok, tokp,
    live_ref, gath_ref, img_ref, cot_ref,
    out_ref, din_ref, grad_ref,
    buf, wqkv, wout, wup, wdn, vec, bup,
    gqkv, gout, gup, gdn, gvec, gbup,
    x_s, dout_s, attn_s, qkv_s, probs_s, mixed_s, dmix_s, dqkv_s,
):
    step = pl.program_id(0)
    window = gath_ref.shape[1]
    weights = (wqkv, wout, wup, wdn)
    grads = (gqkv, gout, gup, gdn)

    @pl.when(step == 0)
    def _():
        for d in range(n):
            first, shift = divmod(shard * d, LANES)
            rows = (shift + shard + LANES - 1) // LANES
            piece = gath_ref[d].astype(F32)
            if d > 0 and shift:
                seam = buf[first : first + 1, :] + piece[0:1]
                buf[first : first + rows, :] = piece[:rows]
                buf[first : first + 1, :] = seam
            else:
                buf[first : first + rows, :] = piece[:rows]
        for k, rows, blocks, start in matrices():
            for b in range(blocks):
                weights[k][:, b * LANES : (b + 1) * LANES] = buf[
                    pl.ds(3 * start + b, rows, blocks), :
                ].astype(BF)
        for i, r in enumerate(VEC_ROWS):
            for c in range(3):
                vec[i : i + 1, c * LANES : (c + 1) * LANES] = buf[3 * r + c : 3 * r + c + 1, :]
        for c in range(FF // LANES):
            bup[:, c * LANES : (c + 1) * LANES] = buf[3 * ROW_BUP + c : 3 * ROW_BUP + c + 1, :]
        for ref in (*grads, gvec, gbup, x_s, dout_s):
            ref[...] = jnp.zeros_like(ref)

    def param(i):
        return vec[i : i + 1, :]

    def add_vec(i, value):
        gvec[i : i + 1, :] += value

    live = live_ref[0]
    masks = [(step * GROUP + g < live).astype(F32) for g in range(GROUP)]
    for g in range(GROUP):
        x_s[g * tokp : g * tokp + tok, :] = img_ref[g].astype(F32)
        dout_s[g * tokp : g * tokp + tok, :] = cot_ref[g].astype(F32) * masks[g]

    hat1, _ = norm_stats(x_s[...])
    attn_s[...] = (hat1 * param(G1) + param(S1)).astype(BF)
    attn_in = attn_s[...]
    for j, bias in enumerate((BQ, None, BV)):
        part = nn(attn_in, wqkv[:, j * D : (j + 1) * D])
        if bias is not None:
            part = part + param(bias)
        qkv_s[:, j * D : (j + 1) * D] = part.astype(BF)

    lane = lax.broadcasted_iota(jnp.int32, (1, LANES), 1)
    low = lane < HD
    low_b = low.astype(BF)
    high_b = 1 - low_b
    key_ok = lax.broadcasted_iota(jnp.int32, (1, tokp), 1) < tok

    def views(t):
        g, p = t // PAIRS, t % PAIRS
        rows = pl.ds(pl.multiple_of(g * tokp, 16), tokp)
        return rows, [pl.ds(pl.multiple_of(j * D + p * LANES, LANES), LANES) for j in range(3)]

    def stack(v):
        return jnp.concatenate([v * low_b, v * high_b], axis=0)

    def attend(t, carry):
        rows, (cq, ck, cv) = views(t)
        q, k, v = qkv_s[rows, cq], qkv_s[rows, ck], qkv_s[rows, cv]
        s = nt(stack(q), k) * (HD**-0.5)
        s = jnp.where(key_ok, s, -1e30)
        e = jnp.exp(s - jnp.max(s, axis=-1, keepdims=True))
        probs = e * (1.0 / jnp.sum(e, axis=-1, keepdims=True))
        probs_s[t] = probs
        mixed = nn(probs.astype(BF), v)
        mixed_s[rows, cq] = jnp.where(low, mixed[:tokp], mixed[tokp:]).astype(BF)
        return carry

    lax.fori_loop(0, GROUP * PAIRS, attend, 0)

    hidden = x_s[...] + nn(mixed_s[...], wout[...]) + param(BO)
    hat2, inv2 = norm_stats(hidden)
    ffn_in = (hat2 * param(G2) + param(S2)).astype(BF)
    dout = dout_s[...]
    dout_b = dout.astype(BF)
    add_vec(BD, colsum(dout))
    result = hidden + param(BD)
    dn2 = jnp.zeros_like(hidden)
    for c in range(FF // CHUNK):
        cols = slice(c * CHUNK, (c + 1) * CHUNK)
        pre = nn(ffn_in, wup[:, cols]) + bup[:, cols]
        cumul = 0.5 * (1.0 + lax.erf(pre * 0.7071067811865476))
        act = (pre * cumul).astype(BF)
        result = result + nn(act, wdn[cols, :])
        gdn[cols, :] += tn(act, dout_b)
        density = jnp.exp(-0.5 * pre * pre) * 0.3989422804014327
        dpre = nt(dout_b, wdn[cols, :]) * (cumul + pre * density)
        gbup[:, cols] += colsum(dpre)
        dpre_b = dpre.astype(BF)
        gup[:, cols] += tn(ffn_in, dpre_b)
        dn2 = dn2 + nt(dpre_b, wup[:, cols])
    for g in range(GROUP):
        out_ref[g] = (result[g * tokp : g * tokp + tok] * masks[g]).astype(BF)

    add_vec(G2, colsum(dn2 * hat2))
    add_vec(S2, colsum(dn2))
    dhidden = dout + norm_back(dn2, hat2, inv2, param(G2))
    dout_s[...] = dhidden
    dhidden_b = dhidden.astype(BF)
    add_vec(BO, colsum(dhidden))
    gout[...] += tn(mixed_s[...], dhidden_b)
    dmix_s[...] = nt(dhidden_b, wout[...]).astype(BF)

    def attend_back(t, carry):
        rows, (cq, ck, cv) = views(t)
        q, k, v = qkv_s[rows, cq], qkv_s[rows, ck], qkv_s[rows, cv]
        dm = stack(dmix_s[rows, cq])
        probs = probs_s[t]
        dprobs = nt(dm, v)
        delta = jnp.sum(probs * dprobs, axis=-1, keepdims=True)
        ds = (probs * (dprobs - delta) * (HD**-0.5)).astype(BF)
        dvalue = tn(probs.astype(BF), dm)
        dq = nn(ds, k)
        dquery = jnp.where(low, dq[:tokp], dq[tokp:])
        dkey = tn(ds, stack(q))
        gvec[BQ : BQ + 1, cq] += colsum(dquery)
        gvec[BV : BV + 1, cq] += colsum(dvalue)
        dqkv_s[rows, cq] = dquery.astype(BF)
        dqkv_s[rows, ck] = dkey.astype(BF)
        dqkv_s[rows, cv] = dvalue.astype(BF)
        return carry

    lax.fori_loop(0, GROUP * PAIRS, attend_back, 0)

    attn_in = attn_s[...]
    dn1 = jnp.zeros_like(hidden)
    for j in range(3):
        cols = slice(j * D, (j + 1) * D)
        part = dqkv_s[:, cols]
        gqkv[:, cols] += tn(attn_in, part)
        dn1 = dn1 + nt(part, wqkv[:, cols])
    hat1, inv1 = norm_stats(x_s[...])
    add_vec(G1, colsum(dn1 * hat1))
    add_vec(S1, colsum(dn1))
    dinput = dout_s[...] + norm_back(dn1, hat1, inv1, param(G1))
    for g in range(GROUP):
        din_ref[g] = dinput[g * tokp : g * tokp + tok].astype(BF)
        dout_s[g * tokp + tok : (g + 1) * tokp, :] = jnp.zeros((tokp - tok, D), F32)

    @pl.when(step == pl.num_programs(0) - 1)
    def _():
        for k, rows, blocks, start in matrices():
            for b in range(blocks):
                buf[pl.ds(3 * start + b, rows, blocks), :] = grads[k][
                    :, b * LANES : (b + 1) * LANES
                ]
        for i, r in enumerate(VEC_ROWS):
            for c in range(3):
                buf[3 * r + c : 3 * r + c + 1, :] = gvec[i : i + 1, c * LANES : (c + 1) * LANES]
        for c in range(FF // LANES):
            buf[3 * ROW_BUP + c : 3 * ROW_BUP + c + 1, :] = gbup[:, c * LANES : (c + 1) * LANES]
        tail = buf.shape[0] - 3 * ROWS
        buf[3 * ROWS :, :] = jnp.zeros((tail, LANES), F32)
        for d in range(n):
            first = shard * d // LANES
            grad_ref[d] = buf[first : first + window, :].astype(grad_ref.dtype)


def run_layer(n, shard, window, live, gathered, images, cotangent):
    slots, tok, _ = images.shape
    tokp = up_to(tok, 16)
    rows = GROUP * tokp
    buf_rows = up_to(max(shard * (n - 1) // LANES + window, 3 * ROWS) + 8, 8)
    block = pl.BlockSpec((GROUP, tok, D), lambda i: (i, 0, 0))
    whole = pl.BlockSpec(memory_space=pltpu.VMEM)
    VM = pltpu.VMEM
    return pl.pallas_call(
        functools.partial(layer_kernel, n, shard, tok, tokp),
        grid=(slots // GROUP,),
        in_specs=[pl.BlockSpec(memory_space=pltpu.SMEM), whole, block, block],
        out_specs=[block, block, whole],
        out_shape=[
            jax.ShapeDtypeStruct(images.shape, BF),
            jax.ShapeDtypeStruct(images.shape, BF),
            jax.ShapeDtypeStruct((n, window, LANES), BF),
        ],
        scratch_shapes=[
            VM((buf_rows, LANES), F32),
            VM((D, 3 * D), BF), VM((D, D), BF), VM((D, FF), BF), VM((FF, D), BF),
            VM((8, D), F32), VM((1, FF), F32),
            VM((D, 3 * D), F32), VM((D, D), F32), VM((D, FF), F32), VM((FF, D), F32),
            VM((8, D), F32), VM((1, FF), F32),
            VM((rows, D), F32), VM((rows, D), F32), VM((rows, D), BF),
            VM((rows, 3 * D), BF), VM((GROUP * PAIRS, 2 * tokp, tokp), F32),
            VM((rows, D), BF), VM((rows, D), BF), VM((rows, 3 * D), BF),
        ],
        compiler_params=pltpu.CompilerParams(
            dimension_semantics=("arbitrary",), vmem_limit_bytes=63 * 1024 * 1024
        ),
        name="layer",
    )(live, gathered, images, cotangent)


PARTS = 4
MESH = pl.DeviceIdType.MESH


def flip(index, mask, bits):
    for b in range(bits):
        if mask >> b & 1:
            index = index + (1 - 2 * (index // (1 << b) % 2)) * (1 << b)
    return index


def part_orders(bits):
    near = list(range(bits))
    swapped = near[:1] + near[2:3] + near[1:2] + near[3:]
    return [near if p % 2 == 0 else swapped for p in range(PARTS)]


def mask_of(k, rest):
    return sum(1 << b for i, b in enumerate(rest) if k >> (len(rest) - 1 - i) & 1)


def greet(me, bits):
    barrier = pltpu.get_barrier_semaphore()
    for b in range(bits):
        pl.semaphore_signal(
            barrier, inc=1, device_id=(flip(me, 1 << b, bits),), device_id_type=MESH
        )
    pl.semaphore_wait(barrier, bits)


def gather_kernel(bits, x_ref, out_ref, send_sem, recv_sem):
    me = lax.axis_index("dp")
    window = x_ref.shape[0]
    part = window // PARTS
    orders = [order[::-1] for order in part_orders(bits)]
    greet(me, bits)
    sends = []

    def copy(p, source, slot, to, first):
        rows = pl.ds(p * part, part)
        return pltpu.make_async_remote_copy(
            src_ref=x_ref.at[rows] if first else out_ref.at[source, rows],
            dst_ref=out_ref.at[source, rows],
            send_sem=send_sem.at[p, slot],
            recv_sem=recv_sem.at[p, slot],
            device_id=(to,),
            device_id_type=MESH,
        )

    def start(p, s):
        order = orders[p]
        to = flip(me, 1 << order[s], bits)
        for k in range(1 << s):
            source = flip(me, mask_of(k, order[:s]), bits)
            c = copy(p, source, (1 << s) - 1 + k, to, k == 0)
            c.start()
            sends.append(c)

    def arrive(p, s):
        order = orders[p]
        to = flip(me, 1 << order[s], bits)
        for k in range(1 << s):
            source = flip(me, mask_of(k, order[:s]) | 1 << order[s], bits)
            copy(p, source, (1 << s) - 1 + k, to, False).wait_recv()

    for p in range(PARTS):
        start(p, 0)
    out_ref[me] = x_ref[...]
    for s in range(bits):
        for p in range(PARTS):
            arrive(p, s)
            if s + 1 < bits:
                start(p, s + 1)
    for c in sends:
        c.wait_send()


def gather(x, n):
    bits = n.bit_length() - 1
    return pl.pallas_call(
        functools.partial(gather_kernel, bits),
        out_shape=jax.ShapeDtypeStruct((n,) + x.shape, x.dtype),
        in_specs=[pl.BlockSpec(memory_space=pltpu.VMEM)],
        out_specs=pl.BlockSpec(memory_space=pltpu.VMEM),
        scratch_shapes=[
            pltpu.SemaphoreType.DMA((PARTS, n - 1)),
            pltpu.SemaphoreType.DMA((PARTS, n - 1)),
        ],
        compiler_params=pltpu.CompilerParams(
            collective_id=1, has_side_effects=True, vmem_limit_bytes=32 * 1024 * 1024
        ),
        name="gather",
    )(x)


def reduce_kernel(bits, g_ref, out_ref, acc, recv, send_sem, recv_sem, first_send, first_recv):
    me = lax.axis_index("dp")
    half = 1 << (bits - 1)
    part = g_ref.shape[1] // PARTS
    orders = part_orders(bits)
    greet(me, bits)
    sends = []

    def first_copy(p, k):
        order = orders[p]
        block = flip(me, mask_of(k, order[1:]) | 1 << order[0], bits)
        return pltpu.make_async_remote_copy(
            src_ref=g_ref.at[block, pl.ds(p * part, part)],
            dst_ref=recv.at[p, k],
            send_sem=first_send.at[p, k],
            recv_sem=first_recv.at[p, k],
            device_id=(flip(me, 1 << order[0], bits),),
            device_id_type=MESH,
        )

    def later_copy(p, s):
        count = half >> s
        base = 2 * half - 2 * count
        return pltpu.make_async_remote_copy(
            src_ref=acc.at[p, pl.ds(count, count)],
            dst_ref=recv.at[p, pl.ds(base, count)],
            send_sem=send_sem.at[p, s],
            recv_sem=recv_sem.at[p, s],
            device_id=(flip(me, 1 << orders[p][s], bits),),
            device_id_type=MESH,
        )

    for p in range(PARTS):
        for k in reversed(range(half)):
            c = first_copy(p, k)
            c.start()
            sends.append(c)
    for s in range(bits):
        count = half >> s
        base = 2 * half - 2 * count
        for p in range(PARTS):
            rows = pl.ds(p * part, part)
            if s == 0:
                for k in reversed(range(half)):
                    first_copy(p, k).wait_recv()
                    own = flip(me, mask_of(k, orders[p][1:]), bits)
                    total = g_ref[own, rows].astype(F32) + recv[p, k].astype(F32)
                    acc[p, k] = total.astype(BF)
                    if k == half // 2:
                        c = later_copy(p, 1)
                        c.start()
                        sends.append(c)
                continue
            later_copy(p, s).wait_recv()
            for k in reversed(range(count)):
                total = acc[p, k].astype(F32) + recv[p, base + k].astype(F32)
                if s + 1 == bits:
                    out_ref[rows, :] = total
                else:
                    acc[p, k] = total.astype(BF)
                    if k == count // 2:
                        c = later_copy(p, s + 1)
                        c.start()
                        sends.append(c)
    for c in sends:
        c.wait_send()


def reduce_windows(grads, n):
    bits = n.bit_length() - 1
    window = grads.shape[1]
    return pl.pallas_call(
        functools.partial(reduce_kernel, bits),
        out_shape=jax.ShapeDtypeStruct((window, LANES), F32),
        in_specs=[pl.BlockSpec(memory_space=pltpu.VMEM)],
        out_specs=pl.BlockSpec(memory_space=pltpu.VMEM),
        scratch_shapes=[
            pltpu.VMEM((PARTS, n // 2, window // PARTS, LANES), BF),
            pltpu.VMEM((PARTS, n, window // PARTS, LANES), BF),
            pltpu.SemaphoreType.DMA((PARTS, bits)),
            pltpu.SemaphoreType.DMA((PARTS, bits)),
            pltpu.SemaphoreType.DMA((PARTS, n // 2)),
            pltpu.SemaphoreType.DMA((PARTS, n // 2)),
        ],
        compiler_params=pltpu.CompilerParams(
            collective_id=2, has_side_effects=True, vmem_limit_bytes=40 * 1024 * 1024
        ),
        name="reduce",
    )(grads)


def shards(params, images, cotangent, live):
    n = lax.axis_size("dp")
    assert n & (n - 1) == 0 and n >= 4
    shard = params.shape[0]
    window = up_to((shard + 2 * LANES - 2) // LANES, 16 * PARTS)
    me = lax.axis_index("dp")
    shift = (shard % LANES) * me % LANES
    padded = jnp.pad(params, (0, window * LANES - shard))
    moved = jnp.roll(padded, shift).astype(BF).reshape(window, LANES)
    gathered = gather(moved, n)
    out, din, grads = run_layer(n, shard, window, live, gathered, images, cotangent)
    mine = reduce_windows(grads, n)
    flat = lax.dynamic_slice(mine.reshape(-1), (shift,), (shard,))
    return out, din, flat


def solution(mesh):
    return jax.shard_map(
        shards,
        mesh=mesh,
        in_specs=(P("dp"), P("dp", None, None), P("dp", None, None), P("dp")),
        out_specs=(P("dp", None, None), P("dp", None, None), P("dp")),
        check_vma=False,
    )
```

```python
import functools

import jax
import jax.numpy as jnp
from jax import lax
from jax.experimental import pallas as pl
from jax.experimental.pallas import tpu as pltpu
from jax.sharding import PartitionSpec as P

D = 384
HEADS = 6
FF = 1536
HD = D // HEADS
PAIRS = HEADS // 2
EPS = 1e-06
LANES = 128
BF = jnp.bfloat16
F32 = jnp.float32

ROW_QKV = 2
ROW_OUT = 2 + 3 * D + 2
ROW_UP = ROW_OUT + D + 3
ROW_BUP = ROW_UP + FF
ROW_DOWN = ROW_BUP + FF // D
ROW_BDOWN = ROW_DOWN + FF
ROWS = ROW_BDOWN + 1
VEC_ROWS = (0, 1, ROW_OUT - 2, ROW_OUT - 1, ROW_UP - 3, ROW_UP - 2, ROW_UP - 1, ROW_BDOWN)
G1, S1, BQ, BV, BO, G2, S2, BD = range(8)

GROUP = 4
CHUNK = 512


def up_to(value, unit):
    return (value + unit - 1) // unit * unit


def nt(a, b):
    return lax.dot_general(a, b, (((1,), (1,)), ((), ())), preferred_element_type=F32)


def tn(a, b):
    return lax.dot_general(a, b, (((0,), (0,)), ((), ())), preferred_element_type=F32)


def nn(a, b):
    return jnp.dot(a, b, preferred_element_type=F32)


def norm_stats(values):
    center = values - jnp.mean(values, axis=-1, keepdims=True)
    inv = lax.rsqrt(jnp.mean(center * center, axis=-1, keepdims=True) + EPS)
    return center * inv, inv


def norm_back(grad_out, hat, inv, gain):
    g = grad_out * gain
    return inv * (
        g
        - jnp.mean(g, axis=-1, keepdims=True)
        - hat * jnp.mean(g * hat, axis=-1, keepdims=True)
    )


def colsum(v):
    return jnp.sum(v, axis=0, keepdims=True)


def matrices():
    return (
        (0, D, 9, ROW_QKV),
        (1, D, 3, ROW_OUT),
        (2, D, 12, ROW_UP),
        (3, FF, 3, ROW_DOWN),
    )


def layer_kernel(
    n, shard, tok, tokp,
    live_ref, gath_ref, img_ref, cot_ref,
    out_ref, din_ref, grad_ref,
    buf, wqkv, wout, wup, wdn, vec, bup,
    gqkv, gout, gup, gdn, gvec, gbup,
    x_s, dout_s, attn_s, qkv_s, probs_s, mixed_s, dmix_s, dqkv_s,
):
    step = pl.program_id(0)
    window = gath_ref.shape[1]
    weights = (wqkv, wout, wup, wdn)
    grads = (gqkv, gout, gup, gdn)

    @pl.when(step == 0)
    def _():
        for d in range(n):
            first, shift = divmod(shard * d, LANES)
            rows = (shift + shard + LANES - 1) // LANES
            piece = gath_ref[d].astype(F32)
            if d > 0 and shift:
                seam = buf[first : first + 1, :] + piece[0:1]
                buf[first : first + rows, :] = piece[:rows]
                buf[first : first + 1, :] = seam
            else:
                buf[first : first + rows, :] = piece[:rows]
        for k, rows, blocks, start in matrices():
            for b in range(blocks):
                weights[k][:, b * LANES : (b + 1) * LANES] = buf[
                    pl.ds(3 * start + b, rows, blocks), :
                ].astype(BF)
        for i, r in enumerate(VEC_ROWS):
            for c in range(3):
                vec[i : i + 1, c * LANES : (c + 1) * LANES] = buf[3 * r + c : 3 * r + c + 1, :]
        for c in range(FF // LANES):
            bup[:, c * LANES : (c + 1) * LANES] = buf[3 * ROW_BUP + c : 3 * ROW_BUP + c + 1, :]
        for ref in (*grads, gvec, gbup, x_s, dout_s):
            ref[...] = jnp.zeros_like(ref)

    def param(i):
        return vec[i : i + 1, :]

    def add_vec(i, value):
        gvec[i : i + 1, :] += value

    live = live_ref[0]
    masks = [(step * GROUP + g < live).astype(F32) for g in range(GROUP)]
    for g in range(GROUP):
        x_s[g * tokp : g * tokp + tok, :] = img_ref[g].astype(F32)
        dout_s[g * tokp : g * tokp + tok, :] = cot_ref[g].astype(F32) * masks[g]

    hat1, _ = norm_stats(x_s[...])
    attn_s[...] = (hat1 * param(G1) + param(S1)).astype(BF)
    attn_in = attn_s[...]
    for j, bias in enumerate((BQ, None, BV)):
        part = nn(attn_in, wqkv[:, j * D : (j + 1) * D])
        if bias is not None:
            part = part + param(bias)
        qkv_s[:, j * D : (j + 1) * D] = part.astype(BF)

    lane = lax.broadcasted_iota(jnp.int32, (1, LANES), 1)
    low = lane < HD
    low_b = low.astype(BF)
    high_b = 1 - low_b
    key_ok = lax.broadcasted_iota(jnp.int32, (1, tokp), 1) < tok

    def views(t):
        g, p = t // PAIRS, t % PAIRS
        rows = pl.ds(pl.multiple_of(g * tokp, 16), tokp)
        return rows, [pl.ds(pl.multiple_of(j * D + p * LANES, LANES), LANES) for j in range(3)]

    def stack(v):
        return jnp.concatenate([v * low_b, v * high_b], axis=0)

    def attend(t, carry):
        rows, (cq, ck, cv) = views(t)
        q, k, v = qkv_s[rows, cq], qkv_s[rows, ck], qkv_s[rows, cv]
        s = nt(stack(q), k) * (HD**-0.5)
        s = jnp.where(key_ok, s, -1e30)
        e = jnp.exp(s - jnp.max(s, axis=-1, keepdims=True))
        probs = e * (1.0 / jnp.sum(e, axis=-1, keepdims=True))
        probs_s[t] = probs
        mixed = nn(probs.astype(BF), v)
        mixed_s[rows, cq] = jnp.where(low, mixed[:tokp], mixed[tokp:]).astype(BF)
        return carry

    lax.fori_loop(0, GROUP * PAIRS, attend, 0)

    hidden = x_s[...] + nn(mixed_s[...], wout[...]) + param(BO)
    hat2, inv2 = norm_stats(hidden)
    ffn_in = (hat2 * param(G2) + param(S2)).astype(BF)
    dout = dout_s[...]
    dout_b = dout.astype(BF)
    add_vec(BD, colsum(dout))
    result = hidden + param(BD)
    dn2 = jnp.zeros_like(hidden)
    for c in range(FF // CHUNK):
        cols = slice(c * CHUNK, (c + 1) * CHUNK)
        pre = nn(ffn_in, wup[:, cols]) + bup[:, cols]
        cumul = 0.5 * (1.0 + lax.erf(pre * 0.7071067811865476))
        act = (pre * cumul).astype(BF)
        result = result + nn(act, wdn[cols, :])
        gdn[cols, :] += tn(act, dout_b)
        density = jnp.exp(-0.5 * pre * pre) * 0.3989422804014327
        dpre = nt(dout_b, wdn[cols, :]) * (cumul + pre * density)
        gbup[:, cols] += colsum(dpre)
        dpre_b = dpre.astype(BF)
        gup[:, cols] += tn(ffn_in, dpre_b)
        dn2 = dn2 + nt(dpre_b, wup[:, cols])
    for g in range(GROUP):
        out_ref[g] = (result[g * tokp : g * tokp + tok] * masks[g]).astype(BF)

    add_vec(G2, colsum(dn2 * hat2))
    add_vec(S2, colsum(dn2))
    dhidden = dout + norm_back(dn2, hat2, inv2, param(G2))
    dout_s[...] = dhidden
    dhidden_b = dhidden.astype(BF)
    add_vec(BO, colsum(dhidden))
    gout[...] += tn(mixed_s[...], dhidden_b)
    dmix_s[...] = nt(dhidden_b, wout[...]).astype(BF)

    def attend_back(t, carry):
        rows, (cq, ck, cv) = views(t)
        q, k, v = qkv_s[rows, cq], qkv_s[rows, ck], qkv_s[rows, cv]
        dm = stack(dmix_s[rows, cq])
        probs = probs_s[t]
        dprobs = nt(dm, v)
        delta = jnp.sum(probs * dprobs, axis=-1, keepdims=True)
        ds = (probs * (dprobs - delta) * (HD**-0.5)).astype(BF)
        dvalue = tn(probs.astype(BF), dm)
        dq = nn(ds, k)
        dquery = jnp.where(low, dq[:tokp], dq[tokp:])
        dkey = tn(ds, stack(q))
        gvec[BQ : BQ + 1, cq] += colsum(dquery)
        gvec[BV : BV + 1, cq] += colsum(dvalue)
        dqkv_s[rows, cq] = dquery.astype(BF)
        dqkv_s[rows, ck] = dkey.astype(BF)
        dqkv_s[rows, cv] = dvalue.astype(BF)
        return carry

    lax.fori_loop(0, GROUP * PAIRS, attend_back, 0)

    attn_in = attn_s[...]
    dn1 = jnp.zeros_like(hidden)
    for j in range(3):
        cols = slice(j * D, (j + 1) * D)
        part = dqkv_s[:, cols]
        gqkv[:, cols] += tn(attn_in, part)
        dn1 = dn1 + nt(part, wqkv[:, cols])
    hat1, inv1 = norm_stats(x_s[...])
    add_vec(G1, colsum(dn1 * hat1))
    add_vec(S1, colsum(dn1))
    dinput = dout_s[...] + norm_back(dn1, hat1, inv1, param(G1))
    for g in range(GROUP):
        din_ref[g] = dinput[g * tokp : g * tokp + tok].astype(BF)
        dout_s[g * tokp + tok : (g + 1) * tokp, :] = jnp.zeros((tokp - tok, D), F32)

    @pl.when(step == pl.num_programs(0) - 1)
    def _():
        for k, rows, blocks, start in matrices():
            for b in range(blocks):
                buf[pl.ds(3 * start + b, rows, blocks), :] = grads[k][
                    :, b * LANES : (b + 1) * LANES
                ]
        for i, r in enumerate(VEC_ROWS):
            for c in range(3):
                buf[3 * r + c : 3 * r + c + 1, :] = gvec[i : i + 1, c * LANES : (c + 1) * LANES]
        for c in range(FF // LANES):
            buf[3 * ROW_BUP + c : 3 * ROW_BUP + c + 1, :] = gbup[:, c * LANES : (c + 1) * LANES]
        tail = buf.shape[0] - 3 * ROWS
        buf[3 * ROWS :, :] = jnp.zeros((tail, LANES), F32)
        for d in range(n):
            first = shard * d // LANES
            grad_ref[d] = buf[first : first + window, :].astype(grad_ref.dtype)


def run_layer(n, shard, window, live, gathered, images, cotangent):
    slots, tok, _ = images.shape
    tokp = up_to(tok, 16)
    rows = GROUP * tokp
    buf_rows = up_to(max(shard * (n - 1) // LANES + window, 3 * ROWS) + 8, 8)
    block = pl.BlockSpec((GROUP, tok, D), lambda i: (i, 0, 0))
    whole = pl.BlockSpec(memory_space=pltpu.VMEM)
    VM = pltpu.VMEM
    return pl.pallas_call(
        functools.partial(layer_kernel, n, shard, tok, tokp),
        grid=(slots // GROUP,),
        in_specs=[pl.BlockSpec(memory_space=pltpu.SMEM), whole, block, block],
        out_specs=[block, block, whole],
        out_shape=[
            jax.ShapeDtypeStruct(images.shape, BF),
            jax.ShapeDtypeStruct(images.shape, BF),
            jax.ShapeDtypeStruct((n, window, LANES), BF),
        ],
        scratch_shapes=[
            VM((buf_rows, LANES), F32),
            VM((D, 3 * D), BF), VM((D, D), BF), VM((D, FF), BF), VM((FF, D), BF),
            VM((8, D), F32), VM((1, FF), F32),
            VM((D, 3 * D), F32), VM((D, D), F32), VM((D, FF), F32), VM((FF, D), F32),
            VM((8, D), F32), VM((1, FF), F32),
            VM((rows, D), F32), VM((rows, D), F32), VM((rows, D), BF),
            VM((rows, 3 * D), BF), VM((GROUP * PAIRS, 2 * tokp, tokp), F32),
            VM((rows, D), BF), VM((rows, D), BF), VM((rows, 3 * D), BF),
        ],
        compiler_params=pltpu.CompilerParams(
            dimension_semantics=("arbitrary",), vmem_limit_bytes=63 * 1024 * 1024
        ),
        name="layer",
    )(live, gathered, images, cotangent)


PARTS = 4
MESH = pl.DeviceIdType.MESH


def flip(index, mask, bits):
    for b in range(bits):
        if mask >> b & 1:
            index = index + (1 - 2 * (index // (1 << b) % 2)) * (1 << b)
    return index


def part_orders(bits):
    near = list(range(bits))
    swapped = near[:1] + near[2:3] + near[1:2] + near[3:]
    orders = [near, swapped]
    for order in (near, swapped):
        orders.append(order[:2] + order[3:4] + order[2:3] + order[4:])
    return orders


def mask_of(k, rest):
    return sum(1 << b for i, b in enumerate(rest) if k >> (len(rest) - 1 - i) & 1)


def greet(me, bits):
    barrier = pltpu.get_barrier_semaphore()
    for b in range(bits):
        pl.semaphore_signal(
            barrier, inc=1, device_id=(flip(me, 1 << b, bits),), device_id_type=MESH
        )
    pl.semaphore_wait(barrier, bits)


def gather_kernel(bits, x_ref, out_ref, send_sem, recv_sem):
    me = lax.axis_index("dp")
    window = x_ref.shape[0]
    part = window // PARTS
    orders = [order[::-1] for order in part_orders(bits)]
    greet(me, bits)
    sends = []

    def copy(p, source, slot, to, first):
        rows = pl.ds(p * part, part)
        return pltpu.make_async_remote_copy(
            src_ref=x_ref.at[rows] if first else out_ref.at[source, rows],
            dst_ref=out_ref.at[source, rows],
            send_sem=send_sem.at[p, slot],
            recv_sem=recv_sem.at[p, slot],
            device_id=(to,),
            device_id_type=MESH,
        )

    def start(p, s):
        order = orders[p]
        to = flip(me, 1 << order[s], bits)
        for k in range(1 << s):
            source = flip(me, mask_of(k, order[:s]), bits)
            c = copy(p, source, (1 << s) - 1 + k, to, k == 0)
            c.start()
            sends.append(c)

    def arrive(p, s):
        order = orders[p]
        to = flip(me, 1 << order[s], bits)
        for k in range(1 << s):
            source = flip(me, mask_of(k, order[:s]) | 1 << order[s], bits)
            copy(p, source, (1 << s) - 1 + k, to, False).wait_recv()

    for p in range(PARTS):
        start(p, 0)
    out_ref[me] = x_ref[...]
    for s in range(bits):
        for p in range(PARTS):
            arrive(p, s)
            if s + 1 < bits:
                start(p, s + 1)
    for c in sends:
        c.wait_send()


def gather(x, n):
    bits = n.bit_length() - 1
    return pl.pallas_call(
        functools.partial(gather_kernel, bits),
        out_shape=jax.ShapeDtypeStruct((n,) + x.shape, x.dtype),
        in_specs=[pl.BlockSpec(memory_space=pltpu.VMEM)],
        out_specs=pl.BlockSpec(memory_space=pltpu.VMEM),
        scratch_shapes=[
            pltpu.SemaphoreType.DMA((PARTS, n - 1)),
            pltpu.SemaphoreType.DMA((PARTS, n - 1)),
        ],
        compiler_params=pltpu.CompilerParams(
            collective_id=1, has_side_effects=True, vmem_limit_bytes=32 * 1024 * 1024
        ),
        name="gather",
    )(x)


def reduce_kernel(bits, g_ref, out_ref, acc, recv, send_sem, recv_sem, first_send, first_recv):
    me = lax.axis_index("dp")
    half = 1 << (bits - 1)
    part = g_ref.shape[1] // PARTS
    orders = part_orders(bits)
    greet(me, bits)
    sends = []

    def first_copy(p, k):
        order = orders[p]
        block = flip(me, mask_of(k, order[1:]) | 1 << order[0], bits)
        return pltpu.make_async_remote_copy(
            src_ref=g_ref.at[block, pl.ds(p * part, part)],
            dst_ref=recv.at[p, k],
            send_sem=first_send.at[p, k],
            recv_sem=first_recv.at[p, k],
            device_id=(flip(me, 1 << order[0], bits),),
            device_id_type=MESH,
        )

    def later_copy(p, s):
        count = half >> s
        base = 2 * half - 2 * count
        return pltpu.make_async_remote_copy(
            src_ref=acc.at[p, pl.ds(count, count)],
            dst_ref=recv.at[p, pl.ds(base, count)],
            send_sem=send_sem.at[p, s],
            recv_sem=recv_sem.at[p, s],
            device_id=(flip(me, 1 << orders[p][s], bits),),
            device_id_type=MESH,
        )

    for p in range(PARTS):
        for k in reversed(range(half)):
            c = first_copy(p, k)
            c.start()
            sends.append(c)
    for s in range(bits):
        count = half >> s
        base = 2 * half - 2 * count
        for p in range(PARTS):
            rows = pl.ds(p * part, part)
            if s == 0:
                for k in reversed(range(half)):
                    first_copy(p, k).wait_recv()
                    own = flip(me, mask_of(k, orders[p][1:]), bits)
                    total = g_ref[own, rows].astype(F32) + recv[p, k].astype(F32)
                    acc[p, k] = total.astype(BF)
                    if k == half // 2:
                        c = later_copy(p, 1)
                        c.start()
                        sends.append(c)
                continue
            later_copy(p, s).wait_recv()
            for k in reversed(range(count)):
                total = acc[p, k].astype(F32) + recv[p, base + k].astype(F32)
                if s + 1 == bits:
                    out_ref[rows, :] = total
                else:
                    acc[p, k] = total.astype(BF)
                    if k == count // 2:
                        c = later_copy(p, s + 1)
                        c.start()
                        sends.append(c)
    for c in sends:
        c.wait_send()


def reduce_windows(grads, n):
    bits = n.bit_length() - 1
    window = grads.shape[1]
    return pl.pallas_call(
        functools.partial(reduce_kernel, bits),
        out_shape=jax.ShapeDtypeStruct((window, LANES), F32),
        in_specs=[pl.BlockSpec(memory_space=pltpu.VMEM)],
        out_specs=pl.BlockSpec(memory_space=pltpu.VMEM),
        scratch_shapes=[
            pltpu.VMEM((PARTS, n // 2, window // PARTS, LANES), BF),
            pltpu.VMEM((PARTS, n, window // PARTS, LANES), BF),
            pltpu.SemaphoreType.DMA((PARTS, bits)),
            pltpu.SemaphoreType.DMA((PARTS, bits)),
            pltpu.SemaphoreType.DMA((PARTS, n // 2)),
            pltpu.SemaphoreType.DMA((PARTS, n // 2)),
        ],
        compiler_params=pltpu.CompilerParams(
            collective_id=2, has_side_effects=True, vmem_limit_bytes=40 * 1024 * 1024
        ),
        name="reduce",
    )(grads)


def shards(params, images, cotangent, live):
    n = lax.axis_size("dp")
    assert n & (n - 1) == 0 and n >= 4
    shard = params.shape[0]
    window = up_to((shard + 2 * LANES - 2) // LANES, 16 * PARTS)
    me = lax.axis_index("dp")
    shift = (shard % LANES) * me % LANES
    padded = jnp.pad(params, (0, window * LANES - shard))
    moved = jnp.roll(padded, shift).astype(BF).reshape(window, LANES)
    gathered = gather(moved, n)
    out, din, grads = run_layer(n, shard, window, live, gathered, images, cotangent)
    mine = reduce_windows(grads, n)
    flat = lax.dynamic_slice(mine.reshape(-1), (shift,), (shard,))
    return out, din, flat


def solution(mesh):
    return jax.shard_map(
        shards,
        mesh=mesh,
        in_specs=(P("dp"), P("dp", None, None), P("dp", None, None), P("dp")),
        out_specs=(P("dp", None, None), P("dp", None, None), P("dp")),
        check_vma=False,
    )
```
